32 devices in a mesh: layer: 2 (over x), trow: 2 (over y), tcol: 8 (over z, core).
Axes of the slice: x: 2, y: 2, z: 4, core: 2. Of those that a mesh axis runs over, the one named last changes fastest.
Arguments:
- act_rows: bfloat16 [2, 1024, 4096], P('layer', ('trow', 'tcol')), may hold values from -6 to 6
- back_rows: bfloat16 [2, 1024, 4096], P('layer', ('trow', 'tcol')), may hold values from -6 to 6
- act_cols: bfloat16 [2, 2048, 4096], P('layer', ('tcol', 'trow')), may hold values from -6 to 6
- back_cols: bfloat16 [2, 2048, 4096], P('layer', ('tcol', 'trow')), may hold values from -6 to 6
Outputs:
- kernel: float32 [1024, 2048], P(('trow', 'layer'), 'tcol')
The draws below stay inside these ranges and needn't reach their ends.
All inputs are finite; a program needn't handle non-finite values.
Results may differ from the reference program's by a relative error of at most 0.0003.
Values may be sent and summed in bfloat16 or wider, within the bound.
A program may use at most 64 MiB of HBM per device.

```python
import jax
import jax.numpy as jnp

D = 4096
LAYERS = 2
ROWS = 1024
COLS = 2048


def shard_levels(rng, extent, pieces, smallest, high):
    def one(position, blocks):
        heights = jax.random.uniform(jax.random.fold_in(jax.random.fold_in(rng, 6), position), (blocks,), jnp.float32, smallest / len(pieces), high / len(pieces))
        return jnp.repeat(jnp.exp(heights), extent[position] // blocks).reshape((-1,) + (1,) * (len(extent) - position - 1))

    loudness = one(*pieces[0])
    for cut in pieces[1:]:
        loudness = loudness * one(*cut)
    return loudness


def scatter_about(key, dims, scale, bound, cuts=(), held_as=jnp.bfloat16):
    entries = jax.random.normal(key, dims, jnp.float32) * scale
    if len(cuts) > 0:
        entries = shard_levels(key, dims, cuts, -0.22, 0.18) * entries
    return jnp.clip(entries, min=-bound, max=bound).astype(held_as)


def setup_inputs(seed: int = 0) -> dict:
    streams_of = jax.random.split(jax.random.key(seed), 5)
    act_rows = scatter_about(streams_of[0], (LAYERS, ROWS, D), 1.0, 6.0, ((0, 2), (1, 16)))
    back_rows = scatter_about(streams_of[1], (LAYERS, ROWS, D), 1.0, 6.0, ((0, 2), (1, 16)))
    act_cols = scatter_about(streams_of[2], (LAYERS, COLS, D), 1.0, 6.0, ((0, 2), (1, 16)))
    back_cols = scatter_about(streams_of[3], (LAYERS, COLS, D), 1.0, 6.0, ((0, 2), (1, 16)))
    return dict(act_rows=act_rows, back_rows=back_rows, act_cols=act_cols, back_cols=back_cols)


def reference(act_rows, back_rows, act_cols, back_cols):
    total = jnp.zeros((ROWS, COLS), jnp.float32)
    for index in range(LAYERS):
        gram_act = jnp.dot(act_rows[index], act_cols[index].T, preferred_element_type=jnp.float32)
        gram_back = jnp.dot(back_rows[index], back_cols[index].T, preferred_element_type=jnp.float32)
        total = total + gram_act * gram_back
    return total / D
```

```python
import functools

import jax
import jax.numpy as jnp
from jax import lax
from jax.experimental import pallas as pl
from jax.experimental.pallas import tpu as pltpu
from jax.sharding import PartitionSpec as P

MESH = pl.DeviceIdType.MESH
CORES = 2


def kernel(sizes, act_rows, back_rows, act_cols, back_cols, out, rows, cols, term, got,
           own_sem, row_recv, up_send, down_send, pair_send, col_send, col_recv, term_send, term_recv):
    layers, trows, tcols, pieces = sizes
    depth = tcols // CORES
    held, width = act_rows.shape[1:]
    part = held // pieces
    strip = act_cols.shape[1]
    share = tcols // layers
    lay, trow, me = lax.axis_index("layer"), lax.axis_index("trow"), lax.axis_index("tcol")
    z, core = me // CORES, me % CORES
    mate = z * CORES + 1 - core
    own_rows, own_cols = (act_rows, back_rows), (act_cols, back_cols)
    chunks = [(a, h) for h in range(pieces) for a in range(2)]

    def up_ok():
        return z + 1 < depth

    def down_ok():
        return z > 0

    barrier = pltpu.get_barrier_semaphore()

    def greet(device):
        pl.semaphore_signal(barrier, inc=1, device_id=device, device_id_type=MESH)

    for step in range(1, layers):
        greet({"layer": lax.rem(lay + step, layers)})
    for step in range(1, trows):
        greet({"trow": lax.rem(trow + step, trows)})
    greet({"tcol": mate})

    @pl.when(up_ok())
    def _():
        greet({"tcol": me + CORES})

    @pl.when(down_ok())
    def _():
        greet({"tcol": me - CORES})

    along = jnp.minimum(z, 1) + jnp.minimum(depth - 1 - z, 1)
    pl.semaphore_wait(barrier, layers + trows - 1 + along)

    def row_copy(origin, a, h, own, send, target):
        src = own_rows[a].at[0, pl.ds(h * part, part)] if own else rows.at[origin, a, pl.ds(h * part, part)]
        slot = a * pieces + h
        return pltpu.make_async_remote_copy(
            src_ref=src,
            dst_ref=rows.at[origin, a, pl.ds(h * part, part)],
            send_sem=send.at[origin, slot],
            recv_sem=row_recv.at[origin, slot],
            device_id={"tcol": target},
            device_id_type=MESH,
        )

    def col_copy(a, step):
        return pltpu.make_async_remote_copy(
            src_ref=own_cols[a].at[0],
            dst_ref=cols.at[a, pl.ds(pl.multiple_of(trow * strip, strip), strip)],
            send_sem=col_send.at[a, step],
            recv_sem=col_recv.at[a, trow],
            device_id={"trow": lax.rem(trow + step, trows)},
            device_id_type=MESH,
        )

    def col_arrival(a, source):
        span = pl.ds(pl.multiple_of(source * strip, strip), strip)
        pltpu.make_async_copy(cols.at[a, span], cols.at[a, span], col_recv.at[a, source]).wait()

    def row_arrival(origin, a, h):
        block = rows.at[origin, a, pl.ds(h * part, part)]
        pltpu.make_async_copy(block, block, row_recv.at[origin, a * pieces + h]).wait()

    def term_copy(origin):
        return pltpu.make_async_remote_copy(
            src_ref=term.at[origin],
            dst_ref=got.at[lay, lax.rem(origin, share)],
            send_sem=term_send.at[origin],
            recv_sem=term_recv.at[lay, lax.rem(origin, share)],
            device_id={"layer": origin // share},
            device_id_type=MESH,
        )

    for a, h in chunks:
        @pl.when(up_ok())
        def _():
            row_copy(me, a, h, True, up_send, me + CORES).start()

        @pl.when(down_ok())
        def _():
            row_copy(me, a, h, True, down_send, me - CORES).start()

    for a in range(2):
        for step in range(1, trows):
            col_copy(a, step).start()
    own = []
    for a in range(2):
        own.append(pltpu.make_async_copy(own_rows[a].at[0], rows.at[me, a], own_sem.at[a]))
        span = pl.ds(pl.multiple_of(trow * strip, strip), strip)
        own.append(pltpu.make_async_copy(own_cols[a].at[0], cols.at[a, span], own_sem.at[2 + a]))
    for copy in own:
        copy.start()
    for a, h in chunks:
        row_copy(me, a, h, True, pair_send, mate).start()

    def compute(origin_z, side):
        origin = origin_z * CORES + side

        @pl.when(side != core)
        def _():
            for a, h in chunks:
                row_arrival(origin, a, h)

        dims = (((1,), (1,)), ((), ()))
        gram_act = lax.dot_general(rows[origin, 0], cols[0], dims, preferred_element_type=jnp.float32)
        gram_back = lax.dot_general(rows[origin, 1], cols[1], dims, preferred_element_type=jnp.float32)
        term[origin] = gram_act * gram_back

        @pl.when(origin // share != lay)
        def _():
            term_copy(origin).start()

    ready = max(1, min(depth - 1, strip * (trows - 1) // held))
    for hop in range(1, depth):
        for a, h in chunks:
            @pl.when(z >= hop)
            def _():
                origin = me - hop * CORES
                row_arrival(origin, a, h)

                @pl.when(up_ok())
                def _():
                    row_copy(origin, a, h, False, up_send, me + CORES).start()

                row_copy(origin, a, h, False, pair_send, mate).start()

            @pl.when(z + hop < depth)
            def _():
                origin = me + hop * CORES
                row_arrival(origin, a, h)

                @pl.when(down_ok())
                def _():
                    row_copy(origin, a, h, False, down_send, me - CORES).start()

                row_copy(origin, a, h, False, pair_send, mate).start()

        if hop == ready:
            for copy in own:
                copy.wait()
            for a in range(2):
                for step in range(1, trows):
                    col_arrival(a, lax.rem(trow + step, trows))

            def first(i, carry):
                origin_z = z - ready + i // CORES

                @pl.when((origin_z >= 0) & (origin_z < depth))
                def _():
                    compute(origin_z, lax.rem(i, CORES))

                return carry

            lax.fori_loop(0, (2 * ready + 1) * CORES, first, 0)
        elif hop > ready:
            def later(i, carry):
                origin_z = z - hop + 2 * hop * (i // CORES)

                @pl.when((origin_z >= 0) & (origin_z < depth))
                def _():
                    compute(origin_z, lax.rem(i, CORES))

                return carry

            lax.fori_loop(0, 2 * CORES, later, 0)

    for b in range(share):
        total = term[lay * share + b]
        for step in range(1, layers):
            source = lax.rem(lay + step, layers)
            slot = got.at[source, b]
            pltpu.make_async_copy(slot, slot, term_recv.at[source, b]).wait()
            total = total + got[source, b]
        out[pl.ds(b * held, held), :] = total / width

    def drain(origin, carry):
        zo, side = origin // CORES, lax.rem(origin, CORES)

        @pl.when(origin // share != lay)
        def _():
            term_copy(origin).wait_send()

        @pl.when(side == core)
        def _():
            for a, h in chunks:
                @pl.when((zo <= z) & up_ok())
                def _():
                    row_copy(origin, a, h, False, up_send, me + CORES).wait_send()

                @pl.when((zo >= z) & down_ok())
                def _():
                    row_copy(origin, a, h, False, down_send, me - CORES).wait_send()

                row_copy(origin, a, h, False, pair_send, mate).wait_send()

        return carry

    lax.fori_loop(0, tcols, drain, 0)
    for a in range(2):
        for step in range(1, trows):
            col_copy(a, step).wait_send()


def local(sizes, act_rows, back_rows, act_cols, back_cols):
    layers, trows, tcols, pieces = sizes
    held, width = act_rows.shape[1:]
    strip = act_cols.shape[1]
    share = tcols // layers
    dma = pltpu.SemaphoreType.DMA
    return pl.pallas_call(
        functools.partial(kernel, sizes),
        out_shape=jax.ShapeDtypeStruct((share * held, trows * strip), jnp.float32),
        in_specs=[pl.BlockSpec(memory_space=pl.ANY)] * 4,
        out_specs=pl.BlockSpec(memory_space=pltpu.VMEM),
        scratch_shapes=[
            pltpu.VMEM((tcols, 2, held, width), act_rows.dtype),
            pltpu.VMEM((2, trows * strip, width), act_cols.dtype),
            pltpu.VMEM((tcols, held, trows * strip), jnp.float32),
            pltpu.VMEM((layers, share, held, trows * strip), jnp.float32),
            dma((4,)),
            dma((tcols, 2 * pieces)),
            dma((tcols, 2 * pieces)),
            dma((tcols, 2 * pieces)),
            dma((tcols, 2 * pieces)),
            dma((2, trows)),
            dma((2, trows)),
            dma((tcols,)),
            dma((layers, share)),
        ],
        compiler_params=pltpu.CompilerParams(
            collective_id=0, has_side_effects=True, vmem_limit_bytes=40 * 1024 * 1024
        ),
    )(act_rows, back_rows, act_cols, back_cols)


def solution(mesh):
    layers, trows, tcols = (mesh.shape[name] for name in ("layer", "trow", "tcol"))
    in_specs = (
        P("layer", ("trow", "tcol"), None),
        P("layer", ("trow", "tcol"), None),
        P("layer", ("tcol", "trow"), None),
        P("layer", ("tcol", "trow"), None),
    )
    out_specs = P(("trow", "layer"), "tcol")

    def body(act_rows, back_rows, act_cols, back_cols):
        held = act_rows.shape[1]
        pieces = 2 if held % 32 == 0 else 1
        return local((layers, trows, tcols, pieces), act_rows, back_rows, act_cols, back_cols)

    return jax.shard_map(body, mesh=mesh, in_specs=in_specs, out_specs=out_specs, check_vma=False)
```

```python
import functools

import jax
import jax.numpy as jnp
from jax import lax
from jax.experimental import pallas as pl
from jax.experimental.pallas import tpu as pltpu
from jax.sharding import PartitionSpec as P

MESH = pl.DeviceIdType.MESH
CORES = 2
TRANS = (((1,), (1,)), ((), ()))


def kernel(sizes, act_rows, back_rows, act_cols, back_cols, out, rows, cols, far, term, got, made, given,
           own_sem, row_recv, up_send, down_send, pair_send, col_send, col_recv, far_send, far_recv,
           made_send, given_recv, term_send, term_recv):
    layers, trows, tcols, pieces, cut = sizes
    depth = tcols // CORES
    held, width = act_rows.shape[1:]
    part = held // pieces
    strip = act_cols.shape[1]
    group = tcols // layers * held
    lay, trow, me = lax.axis_index("layer"), lax.axis_index("trow"), lax.axis_index("tcol")
    z, core = me // CORES, me % CORES
    mate, other = z * CORES + 1 - core, 1 - trow
    own_rows, own_cols = (act_rows, back_rows), (act_cols, back_cols)
    chunks = [(a, h) for h in range(pieces) for a in range(2)]
    edge = (z == 0) | (z == depth - 1)
    inner = (z == 1) | (z == depth - 2)
    inwards = me + CORES - 2 * CORES * jnp.minimum(z, 1)
    outwards = me - CORES + 2 * CORES * jnp.minimum(jnp.maximum(z - 1, 0), 1)

    def up_ok(a):
        return z + 1 + a < depth

    def down_ok(a):
        return z > a

    barrier = pltpu.get_barrier_semaphore()

    def greet(device):
        pl.semaphore_signal(barrier, inc=1, device_id=device, device_id_type=MESH)

    for step in range(1, layers):
        greet({"layer": lax.rem(lay + step, layers)})
    greet({"trow": other})
    greet({"tcol": mate})

    @pl.when(up_ok(0))
    def _():
        greet({"tcol": me + CORES})

    @pl.when(down_ok(0))
    def _():
        greet({"tcol": me - CORES})

    along = jnp.minimum(z, 1) + jnp.minimum(depth - 1 - z, 1)
    pl.semaphore_wait(barrier, layers + 1 + along)

    def remote(src, dst, send, recv, device):
        return pltpu.make_async_remote_copy(
            src_ref=src, dst_ref=dst, send_sem=send, recv_sem=recv, device_id=device, device_id_type=MESH
        )

    def arrival(ref, sem):
        pltpu.make_async_copy(ref, ref, sem).wait()

    def row_block(origin, a, h):
        return rows.at[a, pl.ds(pl.multiple_of(origin * held + h * part, part), part)]

    def row_copy(origin, a, h, own, send, target):
        dst = row_block(origin, a, h)
        src = own_rows[a].at[0, pl.ds(h * part, part)] if own else dst
        slot = a * pieces + h
        return remote(src, dst, send.at[origin, slot], row_recv.at[origin, slot], {"tcol": target})

    def row_arrival(origin, a, h):
        arrival(row_block(origin, a, h), row_recv.at[origin, a * pieces + h])

    def strip_of(t):
        return pl.ds(pl.multiple_of(t * strip, strip), strip)

    def col_copy(a):
        return remote(own_cols[a].at[0], cols.at[a, strip_of(trow)], col_send.at[a], col_recv.at[a], {"trow": other})

    def col_arrival(a):
        arrival(cols.at[a, strip_of(other)], col_recv.at[a])

    lengths = (cut, strip - cut)
    granule = 16

    def span(t, p):
        return pl.ds(pl.multiple_of(t * strip + p * cut, granule), lengths[p])

    def far_own(p, send, device):
        src = back_cols.at[0, pl.ds(p * cut, lengths[p])]
        return remote(src, far.at[span(trow, p)], far_send.at[send], far_recv.at[trow, p], device)

    def far_relay(t, p, send, device):
        block = far.at[span(t, p)]
        return remote(block, block, far_send.at[send], far_recv.at[t, p], device)

    def far_arrival(t, p):
        arrival(far.at[span(t, p)], far_recv.at[t, p])

    def made_copy(d, t, p):
        return remote(made.at[d, span(t, p)], given.at[d, span(t, p)], made_send.at[d, t, p],
                      given_recv.at[d, t, p], {"tcol": outwards})

    def term_copy(d, t, p):
        return remote(term.at[d, span(t, p)], got.at[lay, span(t, p)], term_send.at[d, t, p],
                      term_recv.at[lay, t, p], {"layer": d})

    @pl.when(edge)
    def _():
        far_own(1, 2, {"trow": other}).start()
        far_own(0, 0, {"tcol": inwards}).start()

    for a, h in chunks:
        @pl.when(up_ok(a))
        def _():
            row_copy(me, a, h, True, up_send, me + CORES).start()

        @pl.when(down_ok(a))
        def _():
            row_copy(me, a, h, True, down_send, me - CORES).start()

    @pl.when(edge)
    def _():
        far_own(1, 1, {"tcol": inwards}).start()

    col_copy(0).start()
    own = []
    for a in range(2):
        block = rows.at[a, pl.ds(pl.multiple_of(me * held, held), held)]
        own.append(pltpu.make_async_copy(own_rows[a].at[0], block, own_sem.at[a]))
        own.append(pltpu.make_async_copy(own_cols[a].at[0], cols.at[a, strip_of(trow)], own_sem.at[2 + a]))
    for copy in own:
        copy.start()
    for a, h in chunks:
        if a == 0:
            row_copy(me, a, h, True, pair_send, mate).start()
        else:
            @pl.when(~edge)
            def _():
                row_copy(me, a, h, True, pair_send, mate).start()

    @pl.when(edge)
    def _():
        far_arrival(other, 1)
        far_relay(other, 1, 3, {"tcol": inwards}).start()

    @pl.when(inner)
    def _():
        far_arrival(trow, 0)
        far_relay(trow, 0, 4, {"trow": other}).start()

    @pl.when(~edge)
    def _():
        col_copy(1).start()

    for hop in range(1, depth):
        for a, h in chunks:
            takes = True if a == 0 else ~edge

            @pl.when((z >= hop) & takes)
            def _():
                origin = me - hop * CORES
                row_arrival(origin, a, h)

                @pl.when(up_ok(a))
                def _():
                    row_copy(origin, a, h, False, up_send, me + CORES).start()

                row_copy(origin, a, h, False, pair_send, mate).start()

            @pl.when((z + hop < depth) & takes)
            def _():
                origin = me + hop * CORES
                row_arrival(origin, a, h)

                @pl.when(down_ok(a))
                def _():
                    row_copy(origin, a, h, False, down_send, me - CORES).start()

                row_copy(origin, a, h, False, pair_send, mate).start()

    for copy in own:
        copy.wait()

    def from_mate(i, carry):
        origin = i * CORES + 1 - core
        for h in range(pieces):
            row_arrival(origin, 0, h)

            @pl.when(~edge)
            def _():
                row_arrival(origin, 1, h)

        return carry

    lax.fori_loop(0, depth, from_mate, 0)

    def rows_of(a, d):
        return rows[a, pl.ds(pl.multiple_of(d * group, group), group), :]

    def each_layer(body):
        def step(i, carry):
            body(lax.rem(lay + 1 + i, layers))
            return carry

        lax.fori_loop(0, layers, step, 0)

    def send_term(d, t, p):
        @pl.when(d != lay)
        def _():
            term_copy(d, t, p).start()

    def make_far(t, p):
        def body(d):
            made[d, span(t, p), :] = lax.dot_general(
                far[span(t, p), :], rows_of(1, d), TRANS, preferred_element_type=jnp.float32)
            made_copy(d, t, p).start()

        far_arrival(t, p)
        each_layer(body)

    @pl.when(inner)
    def _():
        def body(d):
            made[d, span(trow, 0), :] = lax.dot_general(
                far[span(trow, 0), :], rows_of(1, d), TRANS, preferred_element_type=jnp.float32)
            made_copy(d, trow, 0).start()

        each_layer(body)
        make_far(other, 0)
        make_far(trow, 1)

    col_arrival(0)

    def gram_act(d):
        term[d] = lax.dot_general(cols[0], rows_of(0, d), TRANS, preferred_element_type=jnp.float32)

    each_layer(gram_act)

    def gram_back(t):
        def body(d):
            strips = strip_of(t)
            term[d, strips, :] = term[d, strips, :] * lax.dot_general(
                cols[1, strips, :], rows_of(1, d), TRANS, preferred_element_type=jnp.float32)
            for p in range(2):
                send_term(d, t, p)

        each_layer(body)

    @pl.when(~edge)
    def _():
        gram_back(trow)

    @pl.when(inner)
    def _():
        make_far(other, 1)

    @pl.when(~edge)
    def _():
        col_arrival(1)
        gram_back(other)

    @pl.when(edge)
    def _():
        for t, p in ((trow, 0), (other, 0), (trow, 1), (other, 1)):
            def body(d):
                block = given.at[d, span(t, p)]
                arrival(block, given_recv.at[d, t, p])
                term[d, span(t, p), :] = term[d, span(t, p), :] * given[d, span(t, p), :]
                send_term(d, t, p)

            each_layer(body)

    for step in range(1, layers):
        source = lax.rem(lay + step, layers)
        for t in range(2):
            for p in range(2):
                arrival(got.at[source, span(t, p)], term_recv.at[source, t, p])
    total = term[lay]
    for step in range(1, layers):
        total = total + got[lax.rem(lay + step, layers)]
    out[...] = total.T / width

    def drain(i, carry):
        origin = i * CORES + core
        for a, h in chunks:
            takes = True if a == 0 else (~edge | (i == z))

            @pl.when((i <= z) & up_ok(a) & takes)
            def _():
                row_copy(origin, a, h, False, up_send, me + CORES).wait_send()

            @pl.when((i >= z) & down_ok(a) & takes)
            def _():
                row_copy(origin, a, h, False, down_send, me - CORES).wait_send()

            if a == 0:
                row_copy(origin, a, h, False, pair_send, mate).wait_send()
            else:
                @pl.when(~edge)
                def _():
                    row_copy(origin, a, h, False, pair_send, mate).wait_send()

        return carry

    lax.fori_loop(0, depth, drain, 0)
    col_copy(0).wait_send()

    @pl.when(~edge)
    def _():
        col_copy(1).wait_send()

    @pl.when(edge)
    def _():
        far_own(0, 0, {"tcol": inwards}).wait_send()
        far_own(1, 1, {"tcol": inwards}).wait_send()
        far_own(1, 2, {"trow": other}).wait_send()
        far_relay(other, 1, 3, {"tcol": inwards}).wait_send()

    @pl.when(inner)
    def _():
        far_relay(trow, 0, 4, {"trow": other}).wait_send()

    def drain_terms(d):
        for t in range(2):
            for p in range(2):
                @pl.when(d != lay)
                def _():
                    term_copy(d, t, p).wait_send()

                @pl.when(inner)
                def _():
                    made_copy(d, t, p).wait_send()

    each_layer(drain_terms)


def local(sizes, act_rows, back_rows, act_cols, back_cols):
    layers, trows, tcols, pieces, cut = sizes
    held, width = act_rows.shape[1:]
    strip = act_cols.shape[1]
    group = tcols // layers * held
    dma = pltpu.SemaphoreType.DMA
    grams = pltpu.VMEM((layers, trows * strip, group), jnp.float32)
    return pl.pallas_call(
        functools.partial(kernel, sizes),
        out_shape=jax.ShapeDtypeStruct((group, trows * strip), jnp.float32),
        in_specs=[pl.BlockSpec(memory_space=pl.ANY)] * 4,
        out_specs=pl.BlockSpec(memory_space=pltpu.VMEM),
        scratch_shapes=[
            pltpu.VMEM((2, tcols * held, width), act_rows.dtype),
            pltpu.VMEM((2, trows * strip, width), act_cols.dtype),
            pltpu.VMEM((trows * strip, width), act_cols.dtype),
            grams, grams, grams, grams,
            dma((4,)),
            dma((tcols, 2 * pieces)),
            dma((tcols, 2 * pieces)),
            dma((tcols, 2 * pieces)),
            dma((tcols, 2 * pieces)),
            dma((2,)),
            dma((2,)),
            dma((5,)),
            dma((2, 2)),
            dma((layers, 2, 2)),
            dma((layers, 2, 2)),
            dma((layers, 2, 2)),
            dma((layers, 2, 2)),
        ],
        compiler_params=pltpu.CompilerParams(
            collective_id=0, has_side_effects=True, vmem_limit_bytes=40 * 1024 * 1024
        ),
    )(act_rows, back_rows, act_cols, back_cols)


def solution(mesh):
    layers, trows, tcols = (mesh.shape[name] for name in ("layer", "trow", "tcol"))
    in_specs = (
        P("layer", ("trow", "tcol"), None),
        P("layer", ("trow", "tcol"), None),
        P("layer", ("tcol", "trow"), None),
        P("layer", ("tcol", "trow"), None),
    )
    out_specs = P(("trow", "layer"), "tcol")

    def body(act_rows, back_rows, act_cols, back_cols):
        held, strip = act_rows.shape[1], act_cols.shape[1]
        pieces = 2 if held % 32 == 0 else 1
        cut = strip // 2
        return local((layers, trows, tcols, pieces, cut), act_rows, back_rows, act_cols, back_cols)

    return jax.shard_map(body, mesh=mesh, in_specs=in_specs, out_specs=out_specs, check_vma=False)
```

```python
import functools

import jax
import jax.numpy as jnp
from jax import lax
from jax.experimental import pallas as pl
from jax.experimental.pallas import tpu as pltpu
from jax.sharding import PartitionSpec as P

MESH = pl.DeviceIdType.MESH
CORES = 2
TRANS = (((1,), (1,)), ((), ()))


def kernel(sizes, act_rows, back_rows, act_cols, back_cols, out, rows, cols, far, term, got, made, given,
           own_sem, row_recv, up_send, down_send, pair_send, col_send, col_recv, far_send, far_recv,
           made_send, given_recv, term_send, term_recv):
    layers, trows, tcols, pieces, cut = sizes
    depth = tcols // CORES
    held, width = act_rows.shape[1:]
    part = held // pieces
    strip = act_cols.shape[1]
    group = tcols // layers * held
    lay, trow, me = lax.axis_index("layer"), lax.axis_index("trow"), lax.axis_index("tcol")
    z, core = me // CORES, me % CORES
    mate, other = z * CORES + 1 - core, 1 - trow
    own_rows, own_cols = (act_rows, back_rows), (act_cols, back_cols)
    chunks = [(a, h) for h in range(pieces) for a in range(2)]
    edge = (z == 0) | (z == depth - 1)
    inner = (z == 1) | (z == depth - 2)
    inwards = me + CORES - 2 * CORES * jnp.minimum(z, 1)
    outwards = me - CORES + 2 * CORES * jnp.minimum(jnp.maximum(z - 1, 0), 1)

    def up_ok(a):
        return z + 1 + a < depth

    def down_ok(a):
        return z > a

    barrier = pltpu.get_barrier_semaphore()

    def greet(device):
        pl.semaphore_signal(barrier, inc=1, device_id=device, device_id_type=MESH)

    for step in range(1, layers):
        greet({"layer": lax.rem(lay + step, layers)})
    greet({"trow": other})
    greet({"tcol": mate})

    @pl.when(up_ok(0))
    def _():
        greet({"tcol": me + CORES})

    @pl.when(down_ok(0))
    def _():
        greet({"tcol": me - CORES})

    along = jnp.minimum(z, 1) + jnp.minimum(depth - 1 - z, 1)
    pl.semaphore_wait(barrier, layers + 1 + along)

    def remote(src, dst, send, recv, device):
        return pltpu.make_async_remote_copy(
            src_ref=src, dst_ref=dst, send_sem=send, recv_sem=recv, device_id=device, device_id_type=MESH
        )

    def arrival(ref, sem):
        pltpu.make_async_copy(ref, ref, sem).wait()

    def row_block(origin, a, h):
        return rows.at[a, pl.ds(pl.multiple_of(origin * held + h * part, part), part)]

    def row_copy(origin, a, h, own, send, target):
        dst = row_block(origin, a, h)
        src = own_rows[a].at[0, pl.ds(h * part, part)] if own else dst
        slot = a * pieces + h
        return remote(src, dst, send.at[origin, slot], row_recv.at[origin, slot], {"tcol": target})

    def row_arrival(origin, a, h):
        arrival(row_block(origin, a, h), row_recv.at[origin, a * pieces + h])

    def strip_of(t):
        return pl.ds(pl.multiple_of(t * strip, strip), strip)

    lengths = (cut, strip - cut)
    granule = 16

    def span(t, p):
        return pl.ds(pl.multiple_of(t * strip + p * cut, granule), lengths[p])

    def col_copy(a, p):
        src = own_cols[a].at[0, pl.ds(p * cut, lengths[p])]
        return remote(src, cols.at[a, span(trow, p)], col_send.at[a, p], col_recv.at[a, p], {"trow": other})

    def col_arrival(a, p):
        arrival(cols.at[a, span(other, p)], col_recv.at[a, p])

    def far_own(p, send, device):
        src = back_cols.at[0, pl.ds(p * cut, lengths[p])]
        return remote(src, far.at[span(trow, p)], far_send.at[send], far_recv.at[trow, p], device)

    def far_relay(t, p, send, device):
        block = far.at[span(t, p)]
        return remote(block, block, far_send.at[send], far_recv.at[t, p], device)

    def far_arrival(t, p):
        arrival(far.at[span(t, p)], far_recv.at[t, p])

    def made_copy(d, t, p):
        return remote(made.at[d, span(t, p)], given.at[d, span(t, p)], made_send.at[d, t, p],
                      given_recv.at[d, t, p], {"tcol": outwards})

    def term_copy(d, t, p):
        return remote(term.at[d, span(t, p)], got.at[lay, span(t, p)], term_send.at[d, t, p],
                      term_recv.at[lay, t, p], {"layer": d})

    @pl.when(edge)
    def _():
        far_own(1, 2, {"trow": other}).start()
        far_own(0, 0, {"tcol": inwards}).start()

    for a, h in chunks:
        @pl.when(up_ok(a))
        def _():
            row_copy(me, a, h, True, up_send, me + CORES).start()

        @pl.when(down_ok(a))
        def _():
            row_copy(me, a, h, True, down_send, me - CORES).start()

    @pl.when(edge)
    def _():
        far_own(1, 1, {"tcol": inwards}).start()

    for p in range(2):
        col_copy(0, p).start()
    own = []
    for a in range(2):
        block = rows.at[a, pl.ds(pl.multiple_of(me * held, held), held)]
        own.append(pltpu.make_async_copy(own_rows[a].at[0], block, own_sem.at[a]))
        own.append(pltpu.make_async_copy(own_cols[a].at[0], cols.at[a, strip_of(trow)], own_sem.at[2 + a]))
    for copy in own:
        copy.start()
    for a, h in chunks:
        if a == 0:
            row_copy(me, a, h, True, pair_send, mate).start()
        else:
            @pl.when(~edge)
            def _():
                row_copy(me, a, h, True, pair_send, mate).start()

    @pl.when(edge)
    def _():
        far_arrival(other, 1)
        far_relay(other, 1, 3, {"tcol": inwards}).start()

    @pl.when(inner)
    def _():
        far_arrival(trow, 0)
        far_relay(trow, 0, 4, {"trow": other}).start()

    @pl.when(~edge)
    def _():
        for p in range(2):
            col_copy(1, p).start()

    for hop in range(1, depth):
        for a, h in chunks:
            takes = True if a == 0 else ~edge

            @pl.when((z >= hop) & takes)
            def _():
                origin = me - hop * CORES
                row_arrival(origin, a, h)

                @pl.when(up_ok(a))
                def _():
                    row_copy(origin, a, h, False, up_send, me + CORES).start()

                row_copy(origin, a, h, False, pair_send, mate).start()

            @pl.when((z + hop < depth) & takes)
            def _():
                origin = me + hop * CORES
                row_arrival(origin, a, h)

                @pl.when(down_ok(a))
                def _():
                    row_copy(origin, a, h, False, down_send, me - CORES).start()

                row_copy(origin, a, h, False, pair_send, mate).start()

    for copy in own:
        copy.wait()

    def from_mate(i, carry):
        origin = i * CORES + 1 - core
        for h in range(pieces):
            row_arrival(origin, 0, h)

            @pl.when(~edge)
            def _():
                row_arrival(origin, 1, h)

        return carry

    lax.fori_loop(0, depth, from_mate, 0)

    def rows_of(a, d):
        return rows[a, pl.ds(pl.multiple_of(d * group, group), group), :]

    def each_layer(body):
        def step(i, carry):
            body(lax.rem(lay + 1 + i, layers))
            return carry

        lax.fori_loop(0, layers, step, 0)

    def send_term(d, t, p):
        @pl.when(d != lay)
        def _():
            term_copy(d, t, p).start()

    def make_far(t, p):
        def body(d):
            made[d, span(t, p), :] = lax.dot_general(
                far[span(t, p), :], rows_of(1, d), TRANS, preferred_element_type=jnp.float32)
            made_copy(d, t, p).start()

        far_arrival(t, p)
        each_layer(body)

    @pl.when(inner)
    def _():
        def body(d):
            made[d, span(trow, 0), :] = lax.dot_general(
                far[span(trow, 0), :], rows_of(1, d), TRANS, preferred_element_type=jnp.float32)
            made_copy(d, trow, 0).start()

        each_layer(body)
        make_far(other, 0)
        make_far(trow, 1)

    for p in range(2):
        col_arrival(0, p)

    def gram_act(d):
        term[d] = lax.dot_general(cols[0], rows_of(0, d), TRANS, preferred_element_type=jnp.float32)

    each_layer(gram_act)

    def gram_back(t, p):
        def body(d):
            strips = span(t, p)
            term[d, strips, :] = term[d, strips, :] * lax.dot_general(
                cols[1, strips, :], rows_of(1, d), TRANS, preferred_element_type=jnp.float32)
            send_term(d, t, p)

        each_layer(body)

    @pl.when(~edge)
    def _():
        for p in range(2):
            gram_back(trow, p)

    @pl.when(inner)
    def _():
        make_far(other, 1)

    @pl.when(~edge)
    def _():
        for p in range(2):
            col_arrival(1, p)
            gram_back(other, p)

    @pl.when(edge)
    def _():
        for t, p in ((trow, 0), (other, 0), (trow, 1), (other, 1)):
            def body(d):
                block = given.at[d, span(t, p)]
                arrival(block, given_recv.at[d, t, p])
                term[d, span(t, p), :] = term[d, span(t, p), :] * given[d, span(t, p), :]
                send_term(d, t, p)

            each_layer(body)

    for step in range(1, layers):
        source = lax.rem(lay + step, layers)
        for t in range(2):
            for p in range(2):
                arrival(got.at[source, span(t, p)], term_recv.at[source, t, p])
    total = term[lay]
    for step in range(1, layers):
        total = total + got[lax.rem(lay + step, layers)]
    out[...] = total.T / width

    def drain(i, carry):
        origin = i * CORES + core
        for a, h in chunks:
            takes = True if a == 0 else (~edge | (i == z))

            @pl.when((i <= z) & up_ok(a) & takes)
            def _():
                row_copy(origin, a, h, False, up_send, me + CORES).wait_send()

            @pl.when((i >= z) & down_ok(a) & takes)
            def _():
                row_copy(origin, a, h, False, down_send, me - CORES).wait_send()

            if a == 0:
                row_copy(origin, a, h, False, pair_send, mate).wait_send()
            else:
                @pl.when(~edge)
                def _():
                    row_copy(origin, a, h, False, pair_send, mate).wait_send()

        return carry

    lax.fori_loop(0, depth, drain, 0)
    for p in range(2):
        col_copy(0, p).wait_send()

    @pl.when(~edge)
    def _():
        for p in range(2):
            col_copy(1, p).wait_send()

    @pl.when(edge)
    def _():
        far_own(0, 0, {"tcol": inwards}).wait_send()
        far_own(1, 1, {"tcol": inwards}).wait_send()
        far_own(1, 2, {"trow": other}).wait_send()
        far_relay(other, 1, 3, {"tcol": inwards}).wait_send()

    @pl.when(inner)
    def _():
        far_relay(trow, 0, 4, {"trow": other}).wait_send()

    def drain_terms(d):
        for t in range(2):
            for p in range(2):
                @pl.when(d != lay)
                def _():
                    term_copy(d, t, p).wait_send()

                @pl.when(inner)
                def _():
                    made_copy(d, t, p).wait_send()

    each_layer(drain_terms)


def local(sizes, act_rows, back_rows, act_cols, back_cols):
    layers, trows, tcols, pieces, cut = sizes
    held, width = act_rows.shape[1:]
    strip = act_cols.shape[1]
    group = tcols // layers * held
    dma = pltpu.SemaphoreType.DMA
    grams = pltpu.VMEM((layers, trows * strip, group), jnp.float32)
    return pl.pallas_call(
        functools.partial(kernel, sizes),
        out_shape=jax.ShapeDtypeStruct((group, trows * strip), jnp.float32),
        in_specs=[pl.BlockSpec(memory_space=pl.ANY)] * 4,
        out_specs=pl.BlockSpec(memory_space=pltpu.VMEM),
        scratch_shapes=[
            pltpu.VMEM((2, tcols * held, width), act_rows.dtype),
            pltpu.VMEM((2, trows * strip, width), act_cols.dtype),
            pltpu.VMEM((trows * strip, width), act_cols.dtype),
            grams, grams, grams, grams,
            dma((4,)),
            dma((tcols, 2 * pieces)),
            dma((tcols, 2 * pieces)),
            dma((tcols, 2 * pieces)),
            dma((tcols, 2 * pieces)),
            dma((2, 2)),
            dma((2, 2)),
            dma((5,)),
            dma((2, 2)),
            dma((layers, 2, 2)),
            dma((layers, 2, 2)),
            dma((layers, 2, 2)),
            dma((layers, 2, 2)),
        ],
        compiler_params=pltpu.CompilerParams(
            collective_id=0, has_side_effects=True, vmem_limit_bytes=62 * 1024 * 1024
        ),
    )(act_rows, back_rows, act_cols, back_cols)


def solution(mesh):
    layers, trows, tcols = (mesh.shape[name] for name in ("layer", "trow", "tcol"))
    in_specs = (
        P("layer", ("trow", "tcol"), None),
        P("layer", ("trow", "tcol"), None),
        P("layer", ("tcol", "trow"), None),
        P("layer", ("tcol", "trow"), None),
    )
    out_specs = P(("trow", "layer"), "tcol")

    def body(act_rows, back_rows, act_cols, back_cols):
        held, strip = act_rows.shape[1], act_cols.shape[1]
        pieces = 2 if held % 32 == 0 else 1
        cut = strip * 5 // 8
        return local((layers, trows, tcols, pieces, cut), act_rows, back_rows, act_cols, back_cols)

    return jax.shard_map(body, mesh=mesh, in_specs=in_specs, out_specs=out_specs, check_vma=False)
```

```python
import functools

import jax
import jax.numpy as jnp
from jax import lax
from jax.experimental import pallas as pl
from jax.experimental.pallas import tpu as pltpu
from jax.sharding import PartitionSpec as P

MESH = pl.DeviceIdType.MESH
CORES = 2
TRANS = (((1,), (1,)), ((), ()))


def kernel(sizes, act_rows, back_rows, act_cols, back_cols, out, rows, cols, far, term, got, made, given,
           own_sem, row_recv, up_send, down_send, pair_send, col_send, col_recv, far_send, far_recv,
           made_send, given_recv, term_send, term_recv):
    layers, trows, tcols, pieces, cut, kept = sizes
    depth = tcols // CORES
    held, width = act_rows.shape[1:]
    part = held // pieces
    strip = act_cols.shape[1]
    group = tcols // layers * held
    lay, trow, me = lax.axis_index("layer"), lax.axis_index("trow"), lax.axis_index("tcol")
    z, core = me // CORES, me % CORES
    mate, other = z * CORES + 1 - core, 1 - trow
    own_rows, own_cols = (act_rows, back_rows), (act_cols, back_cols)
    chunks = [(a, h) for h in range(pieces) for a in range(2)]
    edge = (z == 0) | (z == depth - 1)
    inner = (z == 1) | (z == depth - 2)
    inwards = me + CORES - 2 * CORES * jnp.minimum(z, 1)
    outwards = me - CORES + 2 * CORES * jnp.minimum(jnp.maximum(z - 1, 0), 1)

    barrier = pltpu.get_barrier_semaphore()

    def greet(device):
        pl.semaphore_signal(barrier, inc=1, device_id=device, device_id_type=MESH)

    for step in range(1, layers):
        greet({"layer": lax.rem(lay + step, layers)})
    greet({"trow": other})
    greet({"tcol": mate})

    @pl.when(z + 1 < depth)
    def _():
        greet({"tcol": me + CORES})

    @pl.when(z > 0)
    def _():
        greet({"tcol": me - CORES})

    along = jnp.minimum(z, 1) + jnp.minimum(depth - 1 - z, 1)
    pl.semaphore_wait(barrier, layers + 1 + along)

    def remote(src, dst, send, recv, device):
        return pltpu.make_async_remote_copy(
            src_ref=src, dst_ref=dst, send_sem=send, recv_sem=recv, device_id=device, device_id_type=MESH
        )

    def arrival(ref, sem):
        pltpu.make_async_copy(ref, ref, sem).wait()

    def row_block(origin, a, h, narrow):
        span = pl.ds(pl.multiple_of(origin * held + h * part, part), part)
        return rows.at[a, span, pl.ds(0, kept)] if narrow else rows.at[a, span]

    def row_copy(origin, a, h, own, send, target, narrow):
        dst = row_block(origin, a, h, narrow)
        src = dst
        if own:
            span = pl.ds(h * part, part)
            src = own_rows[a].at[0, span, pl.ds(0, kept)] if narrow else own_rows[a].at[0, span]
        slot = a * pieces + h
        return remote(src, dst, send.at[origin, slot], row_recv.at[origin, slot], {"tcol": target})

    def either(a, full, some, body):
        if a == 0:
            pl.when(full | some)(lambda: body(False))
        else:
            pl.when(full)(lambda: body(False))
            pl.when(some)(lambda: body(True))

    def go(copy, wait):
        copy.wait_send() if wait else copy.start()

    def send_up(origin, a, h, own, wait=False):
        either(a, z + 2 < depth, z + 2 == depth,
               lambda narrow: go(row_copy(origin, a, h, own, up_send, me + CORES, narrow), wait))

    def send_down(origin, a, h, own, wait=False):
        either(a, z > 1, z == 1,
               lambda narrow: go(row_copy(origin, a, h, own, down_send, me - CORES, narrow), wait))

    def send_pair(origin, a, h, own, wait=False):
        either(a, ~edge, edge,
               lambda narrow: go(row_copy(origin, a, h, own, pair_send, mate, narrow), wait))

    def row_arrival(origin, a, h):
        either(a, ~edge, edge,
               lambda narrow: arrival(row_block(origin, a, h, narrow), row_recv.at[origin, a * pieces + h]))

    def strip_of(t):
        return pl.ds(pl.multiple_of(t * strip, strip), strip)

    lengths = (cut, strip - cut)
    granule = 16

    def span(t, p):
        return pl.ds(pl.multiple_of(t * strip + p * cut, granule), lengths[p])

    def col_copy(a, p, deep=width):
        src = own_cols[a].at[0, pl.ds(p * cut, lengths[p]), pl.ds(0, deep)]
        dst = cols.at[a, span(trow, p), pl.ds(0, deep)]
        return remote(src, dst, col_send.at[a, p], col_recv.at[a, p], {"trow": other})

    def col_arrival(a, p, deep=width):
        arrival(cols.at[a, span(other, p), pl.ds(0, deep)], col_recv.at[a, p])

    def far_own(p, send, device):
        src = back_cols.at[0, pl.ds(p * cut, lengths[p]), pl.ds(kept, width - kept)]
        return remote(src, far.at[span(trow, p)], far_send.at[send], far_recv.at[trow, p], device)

    def far_relay(t, p, send, device):
        block = far.at[span(t, p)]
        return remote(block, block, far_send.at[send], far_recv.at[t, p], device)

    def far_arrival(t, p):
        arrival(far.at[span(t, p)], far_recv.at[t, p])

    def made_copy(d, t, p):
        return remote(made.at[d, span(t, p)], given.at[d, span(t, p)], made_send.at[d, t, p],
                      given_recv.at[d, t, p], {"tcol": outwards})

    def term_copy(d, t, p):
        return remote(term.at[d, span(t, p)], got.at[lay, span(t, p)], term_send.at[d, t, p],
                      term_recv.at[lay, t, p], {"layer": d})

    @pl.when(edge)
    def _():
        far_own(1, 2, {"trow": other}).start()
        far_own(0, 0, {"tcol": inwards}).start()

    for a, h in chunks:
        send_up(me, a, h, True)
        send_down(me, a, h, True)

    @pl.when(edge)
    def _():
        far_own(1, 1, {"tcol": inwards}).start()

    for p in range(2):
        col_copy(0, p).start()
    own = []
    for a in range(2):
        block = rows.at[a, pl.ds(pl.multiple_of(me * held, held), held)]
        own.append(pltpu.make_async_copy(own_rows[a].at[0], block, own_sem.at[a]))
        own.append(pltpu.make_async_copy(own_cols[a].at[0], cols.at[a, strip_of(trow)], own_sem.at[2 + a]))
    for copy in own:
        copy.start()
    for a, h in chunks:
        send_pair(me, a, h, True)

    @pl.when(edge)
    def _():
        far_arrival(other, 1)
        far_relay(other, 1, 3, {"tcol": inwards}).start()

    @pl.when(inner)
    def _():
        far_arrival(trow, 0)
        far_relay(trow, 0, 4, {"trow": other}).start()

    @pl.when(~edge)
    def _():
        for p in range(2):
            col_copy(1, p).start()

    @pl.when(edge)
    def _():
        for p in range(2):
            col_copy(1, p, kept).start()

    for hop in range(1, depth):
        for a, h in chunks:
            @pl.when(z >= hop)
            def _():
                origin = me - hop * CORES
                row_arrival(origin, a, h)
                send_up(origin, a, h, False)
                send_pair(origin, a, h, False)

            @pl.when(z + hop < depth)
            def _():
                origin = me + hop * CORES
                row_arrival(origin, a, h)
                send_down(origin, a, h, False)
                send_pair(origin, a, h, False)

    for copy in own:
        copy.wait()

    def from_mate(i, carry):
        origin = i * CORES + 1 - core
        for a, h in chunks:
            row_arrival(origin, a, h)

        return carry

    lax.fori_loop(0, depth, from_mate, 0)

    def rows_of(a, d, start=0, stop=width):
        return rows[a, pl.ds(pl.multiple_of(d * group, group), group), start:stop]

    def each_layer(body):
        def step(i, carry):
            body(lax.rem(lay + 1 + i, layers))
            return carry

        lax.fori_loop(0, layers, step, 0)

    def send_term(d, t, p):
        @pl.when(d != lay)
        def _():
            term_copy(d, t, p).start()

    def make_far(t, p):
        def body(d):
            made[d, span(t, p), :] = lax.dot_general(
                far[span(t, p), :], rows_of(1, d, kept), TRANS, preferred_element_type=jnp.float32)
            made_copy(d, t, p).start()

        far_arrival(t, p)
        each_layer(body)

    @pl.when(inner)
    def _():
        def body(d):
            made[d, span(trow, 0), :] = lax.dot_general(
                far[span(trow, 0), :], rows_of(1, d, kept), TRANS, preferred_element_type=jnp.float32)
            made_copy(d, trow, 0).start()

        each_layer(body)
        make_far(other, 0)
        make_far(trow, 1)

    for p in range(2):
        col_arrival(0, p)

    def gram_act(d):
        term[d] = lax.dot_general(cols[0], rows_of(0, d), TRANS, preferred_element_type=jnp.float32)

    each_layer(gram_act)

    def gram_back(t, p):
        def body(d):
            strips = span(t, p)
            term[d, strips, :] = term[d, strips, :] * lax.dot_general(
                cols[1, strips, :], rows_of(1, d), TRANS, preferred_element_type=jnp.float32)
            send_term(d, t, p)

        each_layer(body)

    @pl.when(~edge)
    def _():
        for p in range(2):
            gram_back(trow, p)

    @pl.when(inner)
    def _():
        make_far(other, 1)

    @pl.when(~edge)
    def _():
        for p in range(2):
            col_arrival(1, p)
            gram_back(other, p)

    @pl.when(edge)
    def _():
        for p in range(2):
            col_arrival(1, p, kept)

        def body(d):
            made[d] = lax.dot_general(
                cols[1, :, :kept], rows_of(1, d, 0, kept), TRANS, preferred_element_type=jnp.float32)

        each_layer(body)
        for t, p in ((trow, 0), (other, 0), (trow, 1), (other, 1)):
            def body(d):
                block = given.at[d, span(t, p)]
                arrival(block, given_recv.at[d, t, p])
                gram = made[d, span(t, p), :] + given[d, span(t, p), :]
                term[d, span(t, p), :] = term[d, span(t, p), :] * gram
                send_term(d, t, p)

            each_layer(body)

    for step in range(1, layers):
        source = lax.rem(lay + step, layers)
        for t in range(2):
            for p in range(2):
                arrival(got.at[source, span(t, p)], term_recv.at[source, t, p])
    total = term[lay]
    for step in range(1, layers):
        total = total + got[lax.rem(lay + step, layers)]
    out[...] = total.T / width

    def drain(i, carry):
        origin = i * CORES + core
        for a, h in chunks:
            pl.when(i <= z)(lambda: send_up(origin, a, h, False, True))
            pl.when(i >= z)(lambda: send_down(origin, a, h, False, True))
            send_pair(origin, a, h, False, True)

        return carry

    lax.fori_loop(0, depth, drain, 0)
    for p in range(2):
        col_copy(0, p).wait_send()

    @pl.when(~edge)
    def _():
        for p in range(2):
            col_copy(1, p).wait_send()

    @pl.when(edge)
    def _():
        for p in range(2):
            col_copy(1, p, kept).wait_send()

    @pl.when(edge)
    def _():
        far_own(0, 0, {"tcol": inwards}).wait_send()
        far_own(1, 1, {"tcol": inwards}).wait_send()
        far_own(1, 2, {"trow": other}).wait_send()
        far_relay(other, 1, 3, {"tcol": inwards}).wait_send()

    @pl.when(inner)
    def _():
        far_relay(trow, 0, 4, {"trow": other}).wait_send()

    def drain_terms(d):
        for t in range(2):
            for p in range(2):
                @pl.when(d != lay)
                def _():
                    term_copy(d, t, p).wait_send()

                @pl.when(inner)
                def _():
                    made_copy(d, t, p).wait_send()

    each_layer(drain_terms)


def local(sizes, act_rows, back_rows, act_cols, back_cols):
    layers, trows, tcols, pieces, cut, kept = sizes
    held, width = act_rows.shape[1:]
    strip = act_cols.shape[1]
    group = tcols // layers * held
    dma = pltpu.SemaphoreType.DMA
    grams = pltpu.VMEM((layers, trows * strip, group), jnp.float32)
    return pl.pallas_call(
        functools.partial(kernel, sizes),
        out_shape=jax.ShapeDtypeStruct((group, trows * strip), jnp.float32),
        in_specs=[pl.BlockSpec(memory_space=pl.ANY)] * 4,
        out_specs=pl.BlockSpec(memory_space=pltpu.VMEM),
        scratch_shapes=[
            pltpu.VMEM((2, tcols * held, width), act_rows.dtype),
            pltpu.VMEM((2, trows * strip, width), act_cols.dtype),
            pltpu.VMEM((trows * strip, width - kept), act_cols.dtype),
            grams, grams, grams, grams,
            dma((4,)),
            dma((tcols, 2 * pieces)),
            dma((tcols, 2 * pieces)),
            dma((tcols, 2 * pieces)),
            dma((tcols, 2 * pieces)),
            dma((2, 2)),
            dma((2, 2)),
            dma((5,)),
            dma((2, 2)),
            dma((layers, 2, 2)),
            dma((layers, 2, 2)),
            dma((layers, 2, 2)),
            dma((layers, 2, 2)),
        ],
        compiler_params=pltpu.CompilerParams(
            collective_id=0, has_side_effects=True, vmem_limit_bytes=62 * 1024 * 1024
        ),
    )(act_rows, back_rows, act_cols, back_cols)


def solution(mesh):
    layers, trows, tcols = (mesh.shape[name] for name in ("layer", "trow", "tcol"))
    in_specs = (
        P("layer", ("trow", "tcol"), None),
        P("layer", ("trow", "tcol"), None),
        P("layer", ("tcol", "trow"), None),
        P("layer", ("tcol", "trow"), None),
    )
    out_specs = P(("trow", "layer"), "tcol")

    def body(act_rows, back_rows, act_cols, back_cols):
        held, strip = act_rows.shape[1], act_cols.shape[1]
        pieces = 2 if held % 32 == 0 else 1
        cut = strip * 5 // 8
        kept = act_rows.shape[2] // 4
        return local((layers, trows, tcols, pieces, cut, kept), act_rows, back_rows, act_cols, back_cols)

    return jax.shard_map(body, mesh=mesh, in_specs=in_specs, out_specs=out_specs, check_vma=False)
```
